256 devices in a mesh: rows: 32 (over x, z_hi, core), cols: 8 (over z_lo, y).
Axes of the slice: x: 4, y: 4, z: 8 (z_hi: 4, z_lo: 2; z = z_hi * 2 + z_lo), core: 2. Of those that a mesh axis runs over, the one named last changes fastest.
Arguments:
- right_side: float32 [4, 8, 1024, 512], P(None, 'cols', 'rows'), may hold values from -6 to 6
- inverse_blocks: bfloat16 [4, 8, 1024, 8192], P(None, None, 'rows', 'cols'), may hold values from -0.09375 to 0.09375
- lower_blocks: bfloat16 [6, 8, 1024, 8192], P(None, None, 'rows', 'cols'), may hold values from -0.046875 to 0.046875
Outputs:
- solution: float32 [4, 8, 1024, 512], P(None, 'cols', 'rows')
The draws below stay inside these ranges and needn't reach their ends.
All inputs are finite; a program needn't handle non-finite values.
Results may differ from the reference program's by a relative error of at most 0.014.
Values may be sent and summed in bfloat16 or wider, within the bound.
A program may use at most 64 MiB of HBM per device.

```python
import jax
import jax.numpy as jnp

PANEL = 8192
NP = 4
NRHS = 512
SUB = 1024
PAIRS = 6
N_COLS = 8


def with_spikes(drawn, own_key, source, target, blocks, factor):
    owner, partner = [(jnp.arange(drawn.shape[axis_at]) // (drawn.shape[axis_at] // blocks)).reshape([-1 if axis == axis_at else 1 for axis in range(drawn.ndim)]) for axis_at in (source, target)]
    chosen = jax.random.permutation(own_key, blocks)[partner]
    strong = (owner == chosen) | (owner == (partner + blocks // 2) % blocks)
    return jnp.where(strong, factor * drawn, drawn)


def block_scale(own_key, dims, shards, least, top_value):
    def one(axis_at, blocks):
        draws = jax.random.uniform(jax.random.fold_in(jax.random.fold_in(own_key, 6), axis_at), (blocks,), jnp.float32, least / len(shards), top_value / len(shards))
        return jnp.repeat(jnp.exp(draws), dims[axis_at] // blocks).reshape((-1,) + (1,) * (len(dims) - axis_at - 1))

    level = one(*shards[0])
    for cut in shards[1:]:
        level = level * one(*cut)
    return level


def bell_draw(stream_key, shape, spread, bound, cuts=(), dtype=jnp.bfloat16):
    result = jax.random.normal(stream_key, shape, jnp.float32) * spread
    if len(cuts) > 0:
        result = block_scale(stream_key, shape, cuts, -0.22, 0.18) * result
    return jnp.clip(result, min=-bound, max=bound).astype(dtype)


def heavy_noise(own_key, dims, width, reach, cuts, heavy, held_as=jnp.bfloat16):
    result = width * jax.random.normal(own_key, dims, jnp.float32)
    if cuts:
        result = result * block_scale(own_key, dims, cuts, -0.22, 0.18)
    return jnp.clip(with_spikes(result, jax.random.fold_in(own_key, 3), *heavy), -reach, reach).astype(held_as)


def setup_inputs(seed: int = 0) -> dict:
    key_list = jax.random.split(jax.random.key(seed), 4)
    return {
        "right_side": bell_draw(key_list[0], (NP, N_COLS, SUB, NRHS), 1.0, 6.0, ((1, 8), (2, 32)), jnp.float32),
        "inverse_blocks": heavy_noise(key_list[1], (NP, N_COLS, SUB, PANEL), PANEL ** -0.5, 0.09375, ((2, 32), (3, 8)), (3, 1, 8, 2.0)),
        "lower_blocks": heavy_noise(key_list[2], (PAIRS, N_COLS, SUB, PANEL), (PANEL * NP) ** -0.5, 0.046875, ((2, 32), (3, 8)), (3, 1, 8, 2.0)),
    }


def pair_index(target, source):
    return target * (target - 1) // 2 + source


def reference(right_side, inverse_blocks, lower_blocks):
    solved_list = []
    rounded_list = []
    for current in range(NP):
        running = jnp.zeros((PANEL, NRHS), jnp.float32)
        for source in range(current):
            factor_block = lower_blocks[pair_index(current, source)].reshape(PANEL, PANEL)
            running = running + jnp.dot(factor_block, rounded_list[source], preferred_element_type=jnp.float32)
        residual = (right_side[current].reshape(PANEL, NRHS) - running).astype(jnp.bfloat16)
        inverse_block = inverse_blocks[current].reshape(PANEL, PANEL)
        solved = jnp.dot(inverse_block, residual, preferred_element_type=jnp.float32)
        solved_list.append(solved.reshape(N_COLS, SUB, NRHS))
        rounded_list.append(solved.astype(jnp.bfloat16))
    return jnp.stack(solved_list)
```

```python
import functools

import jax
import jax.numpy as jnp
from jax import lax
from jax.experimental import pallas as pl
from jax.experimental.pallas import tpu as pltpu
from jax.sharding import PartitionSpec as P

MESH = pl.DeviceIdType.MESH
X, ZH, CORE, ZL, Y = 4, 4, 2, 2, 4
LANES = 128
BF16, F32 = jnp.bfloat16, jnp.float32


def pair_index(target, source):
    return target * (target - 1) // 2 + source


def device(x, zh, core, zl, y):
    return {"rows": (x * ZH + zh) * CORE + core, "cols": zl * Y + y}


def solve_kernel(
    panels, rhs, inv, low, out, fac, bb, g, part, recv, xo, acc, early,
    b_loc, b_send, b_recv, f_loc, f_send, f_recv, rs_send, rs_recv,
    z_send, z_recv, x_send, x_recv, o_loc, o_send, o_recv,
):
    groups = inv.shape[1]
    rows = inv.shape[2]
    block = rows * CORE
    half = rhs.shape[3] // CORE
    chunks = half // LANES
    wide = ZH * block
    height = groups * block

    r = lax.axis_index("rows")
    c = lax.axis_index("cols")
    x, zh, core = r // (ZH * CORE), (r // CORE) % ZH, r % CORE
    zl, y = c // Y, c % Y
    other = 1 - core

    mate = device(x, zh, other, zl, y)
    col_peers = {
        (dz, dy): device(x, zh, core, (zl + dz) % ZL, (y + dy) % Y)
        for dz in range(ZL) for dy in range(Y) if (dz, dy) != (0, 0)
    }
    z_peers = {d: device(x, (zh + d) % ZH, core, zl, y) for d in range(1, ZH)}
    x_peers = {d: device((x + d) % X, zh, core, zl, y) for d in range(1, X)}
    far_cols = sorted(col_peers, key=lambda o: -(o[0] + min(o[1], Y - o[1])))
    far_z = sorted(z_peers, key=lambda d: -min(d, ZH - d))
    far_x = sorted(x_peers, key=lambda d: -min(d, X - d))

    def remote(src, dst, send, recv_sem, peer):
        return pltpu.make_async_remote_copy(
            src_ref=src, dst_ref=dst, send_sem=send, recv_sem=recv_sem,
            device_id=peer, device_id_type=MESH,
        )

    def take(ref, sem):
        pltpu.make_async_copy(ref, ref, sem).wait()

    mine = pl.ds(pl.multiple_of(core * rows, rows), rows)
    theirs = pl.ds(pl.multiple_of(other * rows, rows), rows)
    my_half = pl.ds(pl.multiple_of(core * half, half), half)
    their_half = pl.ds(pl.multiple_of(other * half, half), half)

    def factor_source(f):
        return inv.at[f] if f < panels else low.at[f - panels]

    def rhs_local(p):
        return pltpu.make_async_copy(
            rhs.at[p, 0, :, my_half], bb.at[p, mine, :], b_loc.at[p])

    def rhs_remote(p):
        return remote(
            rhs.at[p, 0, :, their_half], bb.at[p, mine, :],
            b_send.at[p], b_recv.at[p], mate)

    def factor_local(f):
        return pltpu.make_async_copy(factor_source(f), fac.at[f, :, mine, :], f_loc.at[f])

    def factor_remote(f):
        return remote(
            factor_source(f), fac.at[f, :, mine, :], f_send.at[f], f_recv.at[f], mate)

    stages = []
    order = []
    for p in range(panels):
        if p > 0:
            stages.append((p, False))
            order += [panels + pair_index(p, q) for q in reversed(range(p))]
        stages.append((p, True))
        order.append(p)

    rhs_local(0).start()
    factor_local(0).start()
    barrier = pltpu.get_barrier_semaphore()
    everyone = [mate, *col_peers.values(), *z_peers.values(), *x_peers.values()]
    for peer in everyone:
        pl.semaphore_signal(barrier, inc=1, device_id=peer, device_id_type=MESH)
    pl.semaphore_wait(barrier, len(everyone))
    rhs_remote(0).start()
    factor_remote(0).start()

    home = (x * ZH + zh) * block
    here = pl.ds(pl.multiple_of(home, block), block)

    def gather_start(s, h):
        own = g.at[s, h, here, :]
        for d in far_z:
            remote(own, own, z_send.at[s, h], z_recv.at[s, h, d - 1], z_peers[d]).start()
        for d in far_x:
            remote(own, own, x_send.at[s, h], x_recv.at[s, h, d - 1], x_peers[d]).start()

    def gather_relay(s, h):
        for d in far_z[::-1]:
            source = (zh - d) % ZH
            place = pl.ds(pl.multiple_of((x * ZH + source) * block, block), block)
            piece = g.at[s, h, place, :]
            take(piece, z_recv.at[s, h, d - 1])
            for e in far_x:
                remote(piece, piece, x_send.at[s, h], x_recv.at[s, h, e - 1], x_peers[e]).start()

    def plane(d):
        return pl.ds(pl.multiple_of(((x - d) % X) * wide, wide), wide)

    def product(f, s, h, span):
        factor = fac[f, :, :, span].reshape(height, -1)
        return jnp.dot(factor, g[s, h, span, :], preferred_element_type=F32)

    everything = pl.ds(0, X * wide)
    loaded = set()

    def need(f):
        if f not in loaded:
            loaded.add(f)
            factor_local(f).wait()
            take(fac.at[f, :, mine, :], f_recv.at[f])

    def main_factor(s):
        p, inverse = stages[s]
        return p if inverse else panels + pair_index(p, p - 1)

    def relay_and_first(s, h):
        p, inverse = stages[s]
        gather_relay(s, h)
        f = main_factor(s)
        need(f)
        first = product(f, s, h, plane(0))
        if not inverse and p >= 2:
            first = first + early[p - 2, h]
        acc[h] = first

    def finish_product(s, h):
        p, inverse = stages[s]
        f = main_factor(s)
        for d in far_x[::-1]:
            take(g.at[s, h, plane(d), :], x_recv.at[s, h, d - 1])
            acc[h] = acc[h] + product(f, s, h, plane(d))
        part[s, h] = acc[h].astype(BF16)
        for dz, dy in far_cols:
            group = ((zl + dz) % ZL) * Y + (y + dy) % Y
            rows_there = pl.ds(pl.multiple_of(group * block, block), block)
            remote(
                part.at[s, h, rows_there, :], recv.at[s, h, dz * Y + dy],
                rs_send.at[s, h], rs_recv.at[s, h], col_peers[dz, dy],
            ).start()
        if not inverse:
            for later in range(p + 1, panels):
                extra_factor = panels + pair_index(later, p - 1)
                need(extra_factor)
                extra = product(extra_factor, s, h, everything)
                if p > 1:
                    extra = extra + early[later - 2, h]
                early[later - 2, h] = extra

    def out_local(p, h):
        there = pl.ds(pl.multiple_of(core * half + h * LANES, LANES), LANES)
        return pltpu.make_async_copy(
            xo.at[p, h, mine, :], out.at[p, 0, :, there], o_loc.at[p, h])

    def out_remote(p, h):
        there = pl.ds(pl.multiple_of(core * half + h * LANES, LANES), LANES)
        return remote(
            xo.at[p, h, theirs, :], out.at[p, 0, :, there],
            o_send.at[p, h], o_recv.at[p, h], mate)

    def reduce_and_send(s, h):
        p, inverse = stages[s]
        take(recv.at[s, h, pl.ds(1, groups - 1)], rs_recv.at[s, h])
        total = acc[h, pl.ds(pl.multiple_of(c * block, block), block), :]
        for slot in range(1, groups):
            total = total + recv[s, h, slot].astype(F32)
        if inverse:
            xo[p, h] = total
            value = total
        else:
            value = bb[p, :, pl.ds(h * LANES, LANES)] - total
        if s + 1 < len(stages):
            g[s + 1, h, here, :] = value.astype(BF16)
            gather_start(s + 1, h)
        if inverse:
            out_local(p, h).start()
            out_remote(p, h).start()
        take(part.at[s, h, pl.ds(0, (groups - 1) * block), :], rs_send.at[s, h])
        take(g.at[s, h, pl.ds(0, (ZH - 1) * block), :], z_send.at[s, h])
        take(g.at[s, h, pl.ds(0, (X - 1) * wide), :], x_send.at[s, h])

    rhs_local(0).wait()
    take(bb.at[0, mine, :], b_recv.at[0])
    for h in range(chunks):
        g[0, h, here, :] = bb[0, :, pl.ds(h * LANES, LANES)].astype(BF16)
        gather_start(0, h)
    for p in range(1, panels):
        rhs_local(p).start()
        rhs_remote(p).start()
    for f in order[1:]:
        factor_local(f).start()
        factor_remote(f).start()

    for s in range(len(stages)):
        for h in range(chunks):
            relay_and_first(s, h)
        for h in range(chunks):
            finish_product(s, h)
        p, inverse = stages[s]
        if not inverse:
            rhs_local(p).wait()
            take(bb.at[p, mine, :], b_recv.at[p])
        for h in range(chunks):
            reduce_and_send(s, h)

    for p in range(panels):
        rhs_remote(p).wait_send()
        for h in range(chunks):
            out_local(p, h).wait()
            out_remote(p, h).wait_send()
            take(xo.at[p, h, mine, :], o_recv.at[p, h])
    for f in order:
        factor_remote(f).wait_send()


def body(right_side, inverse_blocks, lower_blocks):
    panels, _, rows, columns = right_side.shape
    groups, depth = inverse_blocks.shape[1], inverse_blocks.shape[3]
    factors = panels + lower_blocks.shape[0]
    half = columns // CORE
    chunks = half // LANES
    block = rows * CORE
    steps = 2 * panels - 1
    dma = pltpu.SemaphoreType.DMA
    return pl.pallas_call(
        functools.partial(solve_kernel, panels),
        out_shape=jax.ShapeDtypeStruct(right_side.shape, F32),
        in_specs=[pl.BlockSpec(memory_space=pl.ANY)] * 3,
        out_specs=pl.BlockSpec(memory_space=pl.ANY),
        scratch_shapes=[
            pltpu.VMEM((factors, groups, block, depth), BF16),
            pltpu.VMEM((panels, block, half), F32),
            pltpu.VMEM((steps, chunks, depth, LANES), BF16),
            pltpu.VMEM((steps, chunks, groups * block, LANES), BF16),
            pltpu.VMEM((steps, chunks, groups, block, LANES), BF16),
            pltpu.VMEM((panels, chunks, block, LANES), F32),
            pltpu.VMEM((chunks, groups * block, LANES), F32),
            pltpu.VMEM((panels - 2, chunks, groups * block, LANES), F32),
            dma((panels,)), dma((panels,)), dma((panels,)),
            dma((factors,)), dma((factors,)), dma((factors,)),
            dma((steps, chunks)), dma((steps, chunks)),
            dma((steps, chunks)), dma((steps, chunks, ZH - 1)),
            dma((steps, chunks)), dma((steps, chunks, X - 1)),
            dma((panels, chunks)), dma((panels, chunks)), dma((panels, chunks)),
        ],
        compiler_params=pltpu.CompilerParams(
            collective_id=0, has_side_effects=True, vmem_limit_bytes=40 * 1024 * 1024
        ),
        cost_estimate=pl.CostEstimate(
            flops=2 * factors * groups * rows * depth * columns,
            bytes_accessed=2 * factors * groups * rows * depth, transcendentals=0,
        ),
        name="solve",
    )(right_side, inverse_blocks, lower_blocks)


def solution(mesh):
    return jax.shard_map(
        body,
        mesh=mesh,
        in_specs=(
            P(None, "cols", "rows", None),
            P(None, None, "rows", "cols"),
            P(None, None, "rows", "cols"),
        ),
        out_specs=P(None, "cols", "rows", None),
        check_vma=False,
    )
```
